512 devices in a mesh: sky: 16 (over z_hi, x, core), tm: 32 (over y, z_lo).
Axes of the slice: x: 4, y: 4, z: 16 (z_hi: 2, z_lo: 8; z = z_hi * 8 + z_lo), core: 2. Of those that a mesh axis runs over, the one named last changes fastest.
Arguments:
- attitude: float32 [4, 32, 2048], P(None, 'tm', 'sky'), may hold values from -6 to 6
- slot_time: float32 [4194304], P(('sky', 'tm')), may hold values from -1 to 1
- slot_parallax: float32 [4194304], P(('sky', 'tm')), may hold values from -1 to 1
- slot_observed: float32 [4194304], P(('sky', 'tm')), may hold values from -6 to 6
- slot_phase: float32 [4194304], P(('sky', 'tm')), may hold values from 0 to 1
- slot_knot: int32 [4194304], P(('sky', 'tm')), may hold values from 0 to 2044
- block_source: int32 [131072], P(('sky', 'tm')), may hold values from 0 to 255
- block_count: int32 [131072], P(('sky', 'tm')), may hold values from 1 to 32
- prior: float32 [5, 4096], P(None, ('sky', 'tm')), may hold values from 0.5 to 4
Outputs:
- update: float32 [5, 4096], P(None, ('sky', 'tm'))
The draws below stay inside these ranges and needn't reach their ends.
Inputs may be any that keep to these rules, and one draw needn't show every extreme that they name: The four knots from slot_knot on lie in the transit's time group of 2048 knots. `block_source`: an index into the 256 sources of the block's own sky sector.
All inputs are finite; a program needn't handle non-finite values.
Results may differ from the reference program's by a relative error of at most 0.0003.
Values sent between devices are 32-bit elements; how exact they have to be, the bound alone decides.
No kernel may reach another device: no remote copies, remote signals or barrier semaphores. Data moves between devices by JAX's collectives and lax.ppermute only.
A program may use at most 64 MiB of HBM per device.

```python
import math
import jax
import jax.numpy as jnp
from jax import lax

SLOTS = 32
PARAMS = 5
SRC_SKY = 256
SOURCES = 4096
KNOTS_GROUP = 2048
BLOCKS = 131072
TRANSITS = 4194304
N_SKY = 16
N_TM = 32


def plant(values, key, low, high):
    longest = values.shape.index(max(values.shape))
    spots = []
    for shift in (0, 1):
        where = [jax.random.randint(jax.random.fold_in(key, axis), (), 0, length) for axis, length in enumerate(values.shape)]
        where[longest] = (where[longest] + shift) % values.shape[longest]
        spots.append(tuple(where))
    return values.at[spots[0]].set(low).at[spots[1]].set(high)


def shard_levels(stream_key, extent, cuts, low, top_value):
    loudness, own = 1.0, jax.random.fold_in(stream_key, 6)
    for dim, shards_of in cuts:
        heights = jnp.exp(jax.random.uniform(jax.random.fold_in(own, dim), (shards_of,), jnp.float32, low / len(cuts), top_value / len(cuts)))
        loudness = loudness * jnp.repeat(heights, extent[dim] // shards_of).reshape([-1 if axis == dim else 1 for axis in range(len(extent))])
    return loudness


def centred(key, shape, deviation, reach, shards=(), kind=jnp.bfloat16):
    values = deviation * jax.random.normal(key, shape, jnp.float32)
    if shards:
        values = values * shard_levels(key, shape, shards, -0.22, 0.18)
    return jnp.clip(values, -reach, reach).astype(kind)


def setup_inputs(seed: int = 0) -> dict:
    key_list = jax.random.split(jax.random.key(seed), 10)
    return {
        "attitude": centred(key_list[0], (4, N_TM, KNOTS_GROUP), 1.0, 6.0, ((1, 32), (2, 16)), jnp.float32),
        "slot_time": jnp.clip(jax.random.uniform(key_list[1], (TRANSITS,), jnp.float32, -1.0, 1.0) * shard_levels(key_list[1], (TRANSITS,), ((0, 512),), -0.4, 0.0), -1.0, 1.0),
        "slot_parallax": jnp.clip(jax.random.uniform(key_list[2], (TRANSITS,), jnp.float32, -1.0, 1.0) * shard_levels(key_list[2], (TRANSITS,), ((0, 512),), -0.4, 0.0), -1.0, 1.0),
        "slot_observed": centred(key_list[3], (TRANSITS,), 1.0, 6.0, ((0, 512),), jnp.float32),
        "slot_phase": jnp.clip(1.0 * jax.random.uniform(key_list[4], (TRANSITS,), jnp.float32) ** shard_levels(key_list[4], (TRANSITS,), ((0, 512),), -0.2, 0.2), 0.0, 1.0),
        "slot_knot": plant(jax.random.randint(key_list[5], (TRANSITS,), 0, KNOTS_GROUP - 3), jax.random.fold_in(key_list[5], 1), 0, (KNOTS_GROUP - 3) - 1).astype(jnp.int32),
        "block_source": plant(jax.random.randint(key_list[6], (BLOCKS,), 0, SRC_SKY), jax.random.fold_in(key_list[6], 1), 0, SRC_SKY - 1).astype(jnp.int32),
        "block_count": plant(jax.random.randint(key_list[7], (BLOCKS,), 1, SLOTS + 1), jax.random.fold_in(key_list[7], 1), 1, SLOTS).astype(jnp.int32),
        "prior": jnp.clip(jnp.exp(math.log(4.0) - 2.0794415 * jax.random.uniform(key_list[8], (PARAMS, SOURCES), jnp.float32) ** shard_levels(key_list[8], (PARAMS, SOURCES), ((1, 512),), -0.2, 0.2)), 0.5, 4.0),
    }


PAIR_LIST = [(i, j) for i in range(5) for j in range(i, 5)]

def block_sums(table, knot, phase, time, parallax, observed, count):
    weights = [(1.0 - phase) ** 3 / 6.0, (3.0 * phase ** 3 - 6.0 * phase ** 2 + 4.0) / 6.0, (-3.0 * phase ** 3 + 3.0 * phase ** 2 + 3.0 * phase + 1.0) / 6.0, phase ** 3 / 6.0]
    quat = weights[0][None, :] * table[:, knot]
    for i in range(1, 4):
        quat = quat + weights[i][None, :] * table[:, knot + i]
    cross = quat[0] * quat[0] + quat[1] * quat[1] - quat[2] * quat[2] - quat[3] * quat[3]
    along = 2.0 * (quat[1] * quat[2] + quat[0] * quat[3])
    tilt = 2.0 * (quat[1] * quat[3] - quat[0] * quat[2])
    design = [cross, along, parallax, time * cross, time * along]
    residual = observed - tilt
    rows = [design[i] * design[j] for i, j in PAIR_LIST] + [design[i] * residual for i in range(5)]
    stacked = jnp.stack(rows)
    blocks = count.shape[0]
    stacked = stacked.reshape(20, blocks, -1)
    live = (jnp.arange(stacked.shape[2], dtype=jnp.int32)[None, :] < count[:, None]).astype(stacked.dtype)
    return lax.optimization_barrier(jnp.sum(stacked * live[None], axis=2))

def solve_normals(normal, prior):
    entry = {}
    for index, pair in enumerate(PAIR_LIST):
        entry[pair[1], pair[0]] = normal[index]
    for i in range(5):
        entry[i, i] = entry[i, i] + prior[i]
    lower = {}
    for col in range(5):
        pivot = entry[col, col]
        for k in range(col):
            pivot = pivot - lower[col, k] * lower[col, k]
        root = jnp.sqrt(pivot)
        lower[col, col] = root
        for row in range(col + 1, 5):
            value = entry[row, col]
            for k in range(col):
                value = value - lower[row, k] * lower[col, k]
            lower[row, col] = value / root
    forward = []
    for i in range(5):
        value = normal[15 + i]
        for k in range(i):
            value = value - lower[i, k] * forward[k]
        forward.append(value / lower[i, i])
    result = [None] * 5
    for i in range(4, -1, -1):
        value = forward[i]
        for k in range(i + 1, 5):
            value = value - lower[k, i] * result[k]
        result[i] = value / lower[i, i]
    return jnp.stack(result)

def reference(attitude, slot_time, slot_parallax, slot_observed, slot_phase, slot_knot, block_source, block_count, prior):

    def per_slot(array):
        return array.reshape(N_SKY, N_TM, -1)
    prior_sky = jnp.transpose(prior.reshape(5, N_SKY, SRC_SKY), (1, 0, 2))

    def sector(items):
        knot, phase, time, parallax, observed, source, count, prior_here = items
        sums = jax.vmap(block_sums, in_axes=(1, 0, 0, 0, 0, 0, 0))(attitude, knot, phase, time, parallax, observed, count)
        flat = jnp.transpose(sums, (1, 0, 2)).reshape(20, -1)
        normal = jnp.zeros((20, SRC_SKY), jnp.float32).at[:, source.reshape(-1)].add(flat)
        return solve_normals(normal, prior_here)
    solved = lax.map(sector, (per_slot(slot_knot), per_slot(slot_phase), per_slot(slot_time), per_slot(slot_parallax), per_slot(slot_observed), per_slot(block_source), per_slot(block_count), prior_sky))
    return jnp.transpose(solved, (1, 0, 2)).reshape(5, SOURCES)
```

```python
import jax
import jax.numpy as jnp
from jax import lax
from jax.experimental import pallas as pl
from jax.experimental.pallas import tpu as pltpu
from jax.sharding import PartitionSpec as P

PAIR_LIST = [(i, j) for i in range(5) for j in range(i, 5)]
LANES = 128
SLOTS = 32


def to_slot_rows(tile):
    turned = tile.T
    groups = LANES // SLOTS
    return jnp.concatenate([turned[g * SLOTS : (g + 1) * SLOTS] for g in range(groups)], axis=1)


def prepare_kernel(
    time_ref, parallax_ref, observed_ref, phase_ref, knot_ref, source_ref, count_ref,
    factors_ref, knot_out_ref, low_ref, high_ref,
):
    blocks = factors_ref.shape[2]
    groups = LANES // SLOTS
    per_group = blocks // groups
    row = lax.broadcasted_iota(jnp.int32, (blocks, blocks), 0)
    column = lax.broadcasted_iota(jnp.int32, (blocks, blocks), 1)
    moved = (row == groups * (column % per_group) + column // per_group).astype(jnp.bfloat16)

    def in_order(ref):
        natural = jnp.concatenate([ref[i : i + 1] for i in range(blocks // LANES)], axis=1)
        natural = jnp.broadcast_to(natural.astype(jnp.float32), (8, blocks)).astype(jnp.bfloat16)
        ordered = jnp.dot(natural, moved, preferred_element_type=jnp.float32)
        return (ordered + 0.5).astype(jnp.int32)

    count = in_order(count_ref)[:1]
    source = in_order(source_ref)[:1]
    slot = lax.broadcasted_iota(jnp.int32, (SLOTS, blocks), 0)
    live = (slot < count).astype(jnp.float32)
    u = to_slot_rows(phase_ref[...])
    v = 1.0 - u
    factors_ref[0] = live * (v * v * v / 6.0)
    factors_ref[1] = live * ((3.0 * u * u * u - 6.0 * u * u + 4.0) / 6.0)
    factors_ref[2] = live * ((-3.0 * u * u * u + 3.0 * u * u + 3.0 * u + 1.0) / 6.0)
    factors_ref[3] = live * (u * u * u / 6.0)
    factors_ref[4] = to_slot_rows(time_ref[...])
    factors_ref[5] = live * to_slot_rows(parallax_ref[...])
    factors_ref[6] = to_slot_rows(observed_ref[...])
    knot_out_ref[...] = to_slot_rows(knot_ref[...])
    within = lax.broadcasted_iota(jnp.int32, low_ref.shape, 0)
    low_ref[...] = (source % 8 == within).astype(jnp.float32)
    owner = lax.broadcasted_iota(jnp.int32, high_ref.shape, 0)
    high_ref[...] = (source // 8 == owner).astype(jnp.float32)


def choose(values, bits):
    for bit in bits:
        values = [jnp.where(bit, values[i + 1], values[i]) for i in range(0, len(values), 2)]
    return values[0]


def sums_kernel(table_ref, factors_ref, knot_ref, low_ref, high_ref, out_ref, total_ref):
    rows, comps, _ = table_ref.shape
    blocks = factors_ref.shape[2]
    levels = rows.bit_length() - 1
    total_ref[...] = jnp.zeros_like(total_ref)

    def step(at, half):
        here = (pl.ds(pl.multiple_of(at * 8, 8), 8), pl.ds(half * LANES, LANES))
        knot = knot_ref[here]
        weight = [factors_ref[(i, *here)] for i in range(4)]
        quat = [None] * comps
        spots = []
        for i in range(4):
            k = knot + i
            spots.append((k & (LANES - 1), [((k >> (7 + b)) & 1) == 1 for b in range(levels)]))
        for m in range(comps):
            for i in range(4):
                lane, bits = spots[i]
                found = [
                    jnp.take_along_axis(
                        jnp.broadcast_to(table_ref[s, m : m + 1, :], (8, LANES)), lane, axis=1,
                        mode="promise_in_bounds",
                    )
                    for s in range(rows)
                ]
                term = weight[i] * choose(found, bits)
                quat[m] = term if i == 0 else quat[m] + term
        q0, q1, q2, q3 = quat
        cross = q0 * q0 + q1 * q1 - q2 * q2 - q3 * q3
        along = 2.0 * (q1 * q2 + q0 * q3)
        tilt = 2.0 * (q1 * q3 - q0 * q2)
        time = factors_ref[(4, *here)]
        design = [cross, along, factors_ref[(5, *here)], time * cross, time * along]
        residual = factors_ref[(6, *here)] - tilt
        products = [design[i] * design[j] for i, j in PAIR_LIST]
        products += [design[i] * residual for i in range(5)]
        for p, product in enumerate(products):
            total_ref[p, :, half * LANES : (half + 1) * LANES] += product

    for half in range(blocks // LANES):
        lax.fori_loop(0, SLOTS // 8, lambda at, _, half=half: step(at, half), None)

    low = low_ref[...]
    spread = jnp.concatenate(
        [jnp.sum(total_ref[p], axis=0, keepdims=True) * low for p in range(total_ref.shape[0])], axis=0
    )
    high = high_ref[...].astype(jnp.bfloat16)
    rest = spread
    result = None
    for part in range(3):
        piece = rest.astype(jnp.bfloat16)
        rest = rest - piece.astype(jnp.float32)
        got = lax.dot_general(
            high, piece, (((1,), (1,)), ((), ())), preferred_element_type=jnp.float32
        )
        result = got if part == 0 else result + got
    for j in range(out_ref.shape[0]):
        out_ref[j] = result[j : j + 1]


def solve_kernel(parts_ref, prior_ref, out_ref):
    owned = prior_ref.shape[1]
    total = jnp.sum(parts_ref[...], axis=0)
    normal = [total[:, owned * p : owned * (p + 1)] for p in range(20)]
    entry = {}
    for index, (i, j) in enumerate(PAIR_LIST):
        entry[j, i] = normal[index]
    for i in range(5):
        entry[i, i] = entry[i, i] + prior_ref[i : i + 1, :]
    right = normal[15:]
    lower = {}
    inverse = []
    for col in range(5):
        inverse.append(1.0 / entry[col, col])
        for row in range(col + 1, 5):
            lower[row, col] = entry[row, col] * inverse[col]
        for row in range(col + 1, 5):
            for other in range(col + 1, row + 1):
                entry[row, other] = entry[row, other] - lower[row, col] * entry[other, col]
            right[row] = right[row] - lower[row, col] * right[col]
    result = [None] * 5
    for i in range(4, -1, -1):
        value = right[i] * inverse[i]
        for k in range(i + 1, 5):
            value = value - lower[k, i] * result[k]
        result[i] = value
        out_ref[i : i + 1, :] = value


def on_device(
    attitude,
    slot_time,
    slot_parallax,
    slot_observed,
    slot_phase,
    slot_knot,
    block_source,
    block_count,
    prior,
):
    n_sky = lax.axis_size("sky")
    n_tm = lax.axis_size("tm")
    shard = attitude[:, 0, :]
    blocks = block_source.shape[0]
    owned = prior.shape[1]
    table = lax.all_to_all(
        jnp.broadcast_to(shard[None], (n_sky, *shard.shape)), "sky", 0, 0, tiled=True
    )

    def rows(array):
        return array.reshape(-1, LANES)

    f32 = jnp.float32
    factors, knot, low, high = pl.pallas_call(
        prepare_kernel,
        out_shape=(
            jax.ShapeDtypeStruct((7, SLOTS, blocks), f32),
            jax.ShapeDtypeStruct((SLOTS, blocks), jnp.int32),
            jax.ShapeDtypeStruct((owned, blocks), f32),
            jax.ShapeDtypeStruct((n_tm, blocks), f32),
        ),
        cost_estimate=pl.CostEstimate(flops=1000000, bytes_accessed=500000, transcendentals=0),
        name="prepare",
    )(
        rows(slot_time), rows(slot_parallax), rows(slot_observed), rows(slot_phase), rows(slot_knot),
        rows(block_source), rows(block_count),
    )
    partial = pl.pallas_call(
        sums_kernel,
        out_shape=jax.ShapeDtypeStruct((n_tm, 1, 20 * owned), f32),
        scratch_shapes=[pltpu.VMEM((20, 8, blocks), f32)],
        name="sums",
    )(table, factors, knot, low, high)
    parts = lax.all_to_all(partial, "tm", 0, 0, tiled=True)
    return pl.pallas_call(
        solve_kernel,
        out_shape=jax.ShapeDtypeStruct((5, owned), f32),
        name="solve",
    )(parts, prior)


def solution(mesh):
    in_specs = (
        P(None, "tm", "sky"),
        P(("sky", "tm")),
        P(("sky", "tm")),
        P(("sky", "tm")),
        P(("sky", "tm")),
        P(("sky", "tm")),
        P(("sky", "tm")),
        P(("sky", "tm")),
        P(None, ("sky", "tm")),
    )
    out_specs = P(None, ("sky", "tm"))
    return jax.shard_map(
        on_device, mesh=mesh, in_specs=in_specs, out_specs=out_specs, check_vma=False
    )
```

```python
import jax
import jax.numpy as jnp
from jax import lax
from jax.experimental import pallas as pl
from jax.experimental.pallas import tpu as pltpu
from jax.sharding import PartitionSpec as P

PAIR_LIST = [(i, j) for i in range(5) for j in range(i, 5)]
LANES = 128
SLOTS = 32
SKY_FIRST = 12
TM_FIRST = 22


def to_slot_rows(tile):
    turned = tile.T
    groups = LANES // SLOTS
    return jnp.concatenate([turned[g * SLOTS : (g + 1) * SLOTS] for g in range(groups)], axis=1)


def prepare_kernel(
    time_ref, parallax_ref, observed_ref, phase_ref, knot_ref, source_ref, count_ref,
    factors_ref, knot_out_ref, low_ref, high_ref,
):
    blocks = factors_ref.shape[2]
    groups = LANES // SLOTS
    per_group = blocks // groups
    row = lax.broadcasted_iota(jnp.int32, (blocks, blocks), 0)
    column = lax.broadcasted_iota(jnp.int32, (blocks, blocks), 1)
    moved = (row == groups * (column % per_group) + column // per_group).astype(jnp.bfloat16)

    def in_order(ref):
        natural = jnp.concatenate([ref[i : i + 1] for i in range(blocks // LANES)], axis=1)
        natural = jnp.broadcast_to(natural.astype(jnp.float32), (8, blocks)).astype(jnp.bfloat16)
        ordered = jnp.dot(natural, moved, preferred_element_type=jnp.float32)
        return (ordered + 0.5).astype(jnp.int32)

    count = in_order(count_ref)[:1]
    source = in_order(source_ref)[:1]
    slot = lax.broadcasted_iota(jnp.int32, (SLOTS, blocks), 0)
    live = (slot < count).astype(jnp.float32)
    u = to_slot_rows(phase_ref[...])
    v = 1.0 - u
    factors_ref[0] = live * (v * v * v / 6.0)
    factors_ref[1] = live * ((3.0 * u * u * u - 6.0 * u * u + 4.0) / 6.0)
    factors_ref[2] = live * ((-3.0 * u * u * u + 3.0 * u * u + 3.0 * u + 1.0) / 6.0)
    factors_ref[3] = live * (u * u * u / 6.0)
    factors_ref[4] = to_slot_rows(time_ref[...])
    factors_ref[5] = live * to_slot_rows(parallax_ref[...])
    factors_ref[6] = to_slot_rows(observed_ref[...])
    knot_out_ref[...] = to_slot_rows(knot_ref[...])
    within = lax.broadcasted_iota(jnp.int32, low_ref.shape, 0)
    low_ref[...] = (source % 8 == within).astype(jnp.float32)
    owners = high_ref.shape[0]
    owner = (lax.broadcasted_iota(jnp.int32, high_ref.shape, 0) + TM_FIRST) % owners
    high_ref[...] = (source // 8 == owner).astype(jnp.float32)


def choose(values, bits):
    for bit in bits:
        values = [jnp.where(bit, values[i + 1], values[i]) for i in range(0, len(values), 2)]
    return values[0]


def sums_kernel(table_ref, factors_ref, knot_ref, low_ref, high_ref, out_ref, total_ref):
    rows, comps, _ = table_ref.shape
    blocks = factors_ref.shape[2]
    levels = rows.bit_length() - 1
    total_ref[...] = jnp.zeros_like(total_ref)

    def step(at, half):
        here = (pl.ds(pl.multiple_of(at * 8, 8), 8), pl.ds(half * LANES, LANES))
        knot = knot_ref[here]
        weight = [factors_ref[(i, *here)] for i in range(4)]
        quat = [None] * comps
        spots = []
        for i in range(4):
            k = knot + i
            spots.append((k & (LANES - 1), [((k >> (7 + b)) & 1) == 1 for b in range(levels)]))
        for m in range(comps):
            for i in range(4):
                lane, bits = spots[i]
                found = [
                    jnp.take_along_axis(
                        jnp.broadcast_to(table_ref[(s - SKY_FIRST) % rows, m : m + 1, :], (8, LANES)), lane, axis=1,
                        mode="promise_in_bounds",
                    )
                    for s in range(rows)
                ]
                term = weight[i] * choose(found, bits)
                quat[m] = term if i == 0 else quat[m] + term
        q0, q1, q2, q3 = quat
        cross = q0 * q0 + q1 * q1 - q2 * q2 - q3 * q3
        along = 2.0 * (q1 * q2 + q0 * q3)
        tilt = 2.0 * (q1 * q3 - q0 * q2)
        time = factors_ref[(4, *here)]
        design = [cross, along, factors_ref[(5, *here)], time * cross, time * along]
        residual = factors_ref[(6, *here)] - tilt
        products = [design[i] * design[j] for i, j in PAIR_LIST]
        products += [design[i] * residual for i in range(5)]
        for p, product in enumerate(products):
            total_ref[p, :, half * LANES : (half + 1) * LANES] += product

    for half in range(blocks // LANES):
        lax.fori_loop(0, SLOTS // 8, lambda at, _, half=half: step(at, half), None)

    low = low_ref[...]
    spread = jnp.concatenate(
        [jnp.sum(total_ref[p], axis=0, keepdims=True) * low for p in range(total_ref.shape[0])], axis=0
    )
    high = high_ref[...].astype(jnp.bfloat16)
    rest = spread
    result = None
    for part in range(3):
        piece = rest.astype(jnp.bfloat16)
        rest = rest - piece.astype(jnp.float32)
        got = lax.dot_general(
            high, piece, (((1,), (1,)), ((), ())), preferred_element_type=jnp.float32
        )
        result = got if part == 0 else result + got
    for j in range(out_ref.shape[0]):
        out_ref[j] = result[j : j + 1]


def solve_kernel(parts_ref, prior_ref, out_ref):
    owned = prior_ref.shape[1]
    total = jnp.sum(parts_ref[...], axis=0)
    normal = [total[:, owned * p : owned * (p + 1)] for p in range(20)]
    entry = {}
    for index, (i, j) in enumerate(PAIR_LIST):
        entry[j, i] = normal[index]
    for i in range(5):
        entry[i, i] = entry[i, i] + prior_ref[i : i + 1, :]
    right = normal[15:]
    lower = {}
    inverse = []
    for col in range(5):
        inverse.append(1.0 / entry[col, col])
        for row in range(col + 1, 5):
            lower[row, col] = entry[row, col] * inverse[col]
        for row in range(col + 1, 5):
            for other in range(col + 1, row + 1):
                entry[row, other] = entry[row, other] - lower[row, col] * entry[other, col]
            right[row] = right[row] - lower[row, col] * right[col]
    result = [None] * 5
    for i in range(4, -1, -1):
        value = right[i] * inverse[i]
        for k in range(i + 1, 5):
            value = value - lower[k, i] * result[k]
        result[i] = value
        out_ref[i : i + 1, :] = value


def exchanged(array, axis, first):
    peers = lax.axis_size(axis)
    order = [(first + i) % peers for i in range(peers)]
    return lax.all_to_all(array, axis, 0, 0, axis_index_groups=[order], tiled=True)


def on_device(
    attitude,
    slot_time,
    slot_parallax,
    slot_observed,
    slot_phase,
    slot_knot,
    block_source,
    block_count,
    prior,
):
    n_sky = lax.axis_size("sky")
    n_tm = lax.axis_size("tm")
    shard = attitude[:, 0, :]
    blocks = block_source.shape[0]
    owned = prior.shape[1]
    table = exchanged(jnp.broadcast_to(shard[None], (n_sky, *shard.shape)), "sky", SKY_FIRST)

    def rows(array):
        return array.reshape(-1, LANES)

    f32 = jnp.float32
    factors, knot, low, high = pl.pallas_call(
        prepare_kernel,
        out_shape=(
            jax.ShapeDtypeStruct((7, SLOTS, blocks), f32),
            jax.ShapeDtypeStruct((SLOTS, blocks), jnp.int32),
            jax.ShapeDtypeStruct((owned, blocks), f32),
            jax.ShapeDtypeStruct((n_tm, blocks), f32),
        ),
        cost_estimate=pl.CostEstimate(flops=1000000, bytes_accessed=500000, transcendentals=0),
        name="prepare",
    )(
        rows(slot_time), rows(slot_parallax), rows(slot_observed), rows(slot_phase), rows(slot_knot),
        rows(block_source), rows(block_count),
    )
    partial = pl.pallas_call(
        sums_kernel,
        out_shape=jax.ShapeDtypeStruct((n_tm, 1, 20 * owned), f32),
        scratch_shapes=[pltpu.VMEM((20, 8, blocks), f32)],
        name="sums",
    )(table, factors, knot, low, high)
    parts = exchanged(partial, "tm", TM_FIRST)
    return pl.pallas_call(
        solve_kernel,
        out_shape=jax.ShapeDtypeStruct((5, owned), f32),
        name="solve",
    )(parts, prior)


def solution(mesh):
    in_specs = (
        P(None, "tm", "sky"),
        P(("sky", "tm")),
        P(("sky", "tm")),
        P(("sky", "tm")),
        P(("sky", "tm")),
        P(("sky", "tm")),
        P(("sky", "tm")),
        P(("sky", "tm")),
        P(None, ("sky", "tm")),
    )
    out_specs = P(None, ("sky", "tm"))
    return jax.shard_map(
        on_device, mesh=mesh, in_specs=in_specs, out_specs=out_specs, check_vma=False
    )
```

```python
import jax
import jax.numpy as jnp
from jax import lax
from jax.experimental import pallas as pl
from jax.experimental.pallas import tpu as pltpu
from jax.sharding import PartitionSpec as P

PAIR_LIST = [(i, j) for i in range(5) for j in range(i, 5)]
LANES = 128
SLOTS = 32
COMPS = 4
PAIRS = 6
SKY_FIRST = 12
TM_FIRST = 22


def to_slot_rows(tile):
    turned = tile.T
    groups = LANES // SLOTS
    return jnp.concatenate([turned[g * SLOTS : (g + 1) * SLOTS] for g in range(groups)], axis=1)


def prepare_kernel(
    phase_in, knot_in, source_in, count_in, time_in, parallax_in, observed_in,
    octet_ref, weight_ref, extra_ref, low_ref, high_ref,
    phase_ref, knot_ref, source_ref, count_ref, time_ref, parallax_ref, observed_ref, sems,
):
    pairs = (
        (count_in, count_ref), (source_in, source_ref), (phase_in, phase_ref), (knot_in, knot_ref),
        (time_in, time_ref), (parallax_in, parallax_ref), (observed_in, observed_ref),
    )
    copies = [pltpu.make_async_copy(a, b, sems.at[i]) for i, (a, b) in enumerate(pairs)]
    for copy in copies:
        copy.start()
    for copy in copies:
        copy.wait()
    blocks = octet_ref.shape[1]
    groups = LANES // SLOTS
    per_group = blocks // groups
    row = lax.broadcasted_iota(jnp.int32, (blocks, blocks), 0)
    column = lax.broadcasted_iota(jnp.int32, (blocks, blocks), 1)
    moved = (row == groups * (column % per_group) + column // per_group).astype(jnp.bfloat16)

    def in_order(ref):
        natural = jnp.concatenate([ref[i : i + 1] for i in range(blocks // LANES)], axis=1)
        natural = jnp.broadcast_to(natural.astype(jnp.float32), (8, blocks)).astype(jnp.bfloat16)
        ordered = jnp.dot(natural, moved, preferred_element_type=jnp.float32)
        return (ordered + 0.5).astype(jnp.int32)

    count = in_order(count_ref)[:1]
    source = in_order(source_ref)[:1]
    slot = lax.broadcasted_iota(jnp.int32, (SLOTS, blocks), 0)
    live = (slot < count).astype(jnp.float32)
    extra_ref[0] = to_slot_rows(time_ref[...])
    extra_ref[1] = to_slot_rows(parallax_ref[...]) * live
    extra_ref[2] = to_slot_rows(observed_ref[...])
    owned = low_ref.shape[0]
    within = lax.broadcasted_iota(jnp.int32, low_ref.shape, 0)
    low_ref[...] = (source % owned == within).astype(jnp.float32)
    owners = high_ref.shape[0]
    owner = (lax.broadcasted_iota(jnp.int32, high_ref.shape, 0) + TM_FIRST) % owners
    high_ref[...] = (source // owned == owner).astype(jnp.float32)

    u = to_slot_rows(phase_ref[...])
    v = 1.0 - u
    weights = [
        live * (v * v * v / 6.0),
        live * ((3.0 * u * u * u - 6.0 * u * u + 4.0) / 6.0),
        live * ((-3.0 * u * u * u + 3.0 * u * u + 3.0 * u + 1.0) / 6.0),
        live * (u * u * u / 6.0),
    ]
    knot = to_slot_rows(knot_ref[...])
    start = knot & 7
    octet_ref[...] = (knot >> 3).astype(jnp.float32)
    later = lax.broadcasted_iota(jnp.int32, (8, blocks), 0) // COMPS
    for s in range(SLOTS):
        ahead = later - start[s : s + 1]
        for a in range(PAIRS):
            value = jnp.zeros((8, blocks), jnp.float32)
            for i in range(4):
                value = jnp.where(ahead == i - 2 * a, weights[i][s : s + 1], value)
            weight_ref[s, 8 * a : 8 * a + 8] = value


def octet_rows(table_ref):
    parts = table_ref.shape[0]
    lane = lax.broadcasted_iota(jnp.int32, (8, LANES), 1)
    sub = lax.broadcasted_iota(jnp.int32, (8, LANES), 0)
    pairs = [
        jnp.concatenate([table_ref[(2 * v + p - SKY_FIRST) % parts] for p in range(2)], axis=0)
        for v in range(parts // 2)
    ]
    in_place = (lane // 16) % 2 == sub // COMPS
    halves = []
    for h in range(2):
        wide = []
        for j in range(8):
            spot = 8 * (lane % 16) + j
            found = [
                jnp.take_along_axis(pairs[4 * h + q], spot, axis=1, mode="promise_in_bounds")
                for q in range(4)
            ]
            chosen = found[0]
            for q in range(1, 4):
                chosen = jnp.where(lane // 32 == q, found[q], chosen)
            wide.append(jnp.where(in_place, chosen, pltpu.roll(chosen, COMPS, 0)))
        halves.append([jnp.where(sub < COMPS, wide[2 * a], wide[2 * a + 1]) for a in range(4)])
    rows = []
    for a in range(4):
        rows.append(jnp.concatenate([halves[0][a], halves[1][a]], axis=1))
    for a in range(2):
        moved = [pltpu.roll(halves[h][a], LANES - 1, 1) for h in range(2)]
        rows.append(
            jnp.concatenate(
                [jnp.where(lane == LANES - 1, moved[1 - h], moved[h]) for h in range(2)], axis=1
            )
        )
    return jnp.concatenate(rows, axis=0)


def in_three(array):
    pieces = []
    for _ in range(3):
        pieces.append(array.astype(jnp.bfloat16))
        array = array - pieces[-1].astype(jnp.float32)
    return pieces


def sums_kernel(
    table_ref, octet_ref, weight_ref, extra_ref, low_ref, high_ref,
    out_ref, quat_ref,
):
    blocks = octet_ref.shape[1]
    high_rows = 8 * PAIRS
    table = jnp.concatenate(in_three(octet_rows(table_ref)), axis=0)
    octets = table.shape[1]
    numbers = lax.broadcasted_iota(jnp.int32, (octets, blocks), 0).astype(jnp.float32).astype(jnp.bfloat16)
    one, zero = jnp.bfloat16(1.0), jnp.bfloat16(0.0)
    for s in range(SLOTS):
        here = jnp.broadcast_to(octet_ref[s : s + 1, :], (16, blocks)).astype(jnp.bfloat16)
        here = jnp.concatenate([here] * (octets // 16), axis=0)
        pick = jnp.where(numbers == here, one, zero)
        got = jnp.dot(table, pick, preferred_element_type=jnp.float32)
        got = got[:high_rows] + got[high_rows : 2 * high_rows] + got[2 * high_rows :]
        got = got * weight_ref[s]
        both = got[:8]
        for a in range(1, PAIRS):
            both = both + got[8 * a : 8 * a + 8]
        both = both + pltpu.roll(both, COMPS, 0)
        for m in range(COMPS):
            quat_ref[m, s : s + 1, :] = both[m : m + 1]

    totals = [None] * 20
    for at in range(SLOTS // 8):
        here = slice(8 * at, 8 * at + 8)
        q0, q1, q2, q3 = (quat_ref[m, here, :] for m in range(COMPS))
        cross = q0 * q0 + q1 * q1 - q2 * q2 - q3 * q3
        along = 2.0 * (q1 * q2 + q0 * q3)
        tilt = 2.0 * (q1 * q3 - q0 * q2)
        time = extra_ref[0, here, :]
        design = [cross, along, extra_ref[1, here, :], time * cross, time * along]
        residual = extra_ref[2, here, :] - tilt
        products = [design[i] * design[j] for i, j in PAIR_LIST]
        products += [design[i] * residual for i in range(5)]
        totals = [p if t is None else t + p for t, p in zip(totals, products)]

    low = low_ref[...]
    spread = jnp.concatenate([jnp.sum(t, axis=0, keepdims=True) * low for t in totals], axis=0)
    high = high_ref[...].astype(jnp.bfloat16)
    result = None
    for piece in in_three(spread):
        got = lax.dot_general(
            high, piece, (((1,), (1,)), ((), ())), preferred_element_type=jnp.float32
        )
        result = got if result is None else result + got
    for j in range(out_ref.shape[0]):
        out_ref[j] = result[j : j + 1]


def solve_kernel(parts_ref, prior_ref, out_ref):
    owned = prior_ref.shape[1]
    total = jnp.sum(parts_ref[...], axis=0)
    normal = [total[:, owned * p : owned * (p + 1)] for p in range(20)]
    entry = {}
    for index, (i, j) in enumerate(PAIR_LIST):
        entry[j, i] = normal[index]
    for i in range(5):
        entry[i, i] = entry[i, i] + prior_ref[i : i + 1, :]
    right = normal[15:]
    lower = {}
    inverse = []
    for col in range(5):
        inverse.append(1.0 / entry[col, col])
        for row in range(col + 1, 5):
            lower[row, col] = entry[row, col] * inverse[col]
        for row in range(col + 1, 5):
            for other in range(col + 1, row + 1):
                entry[row, other] = entry[row, other] - lower[row, col] * entry[other, col]
            right[row] = right[row] - lower[row, col] * right[col]
    result = [None] * 5
    for i in range(4, -1, -1):
        value = right[i] * inverse[i]
        for k in range(i + 1, 5):
            value = value - lower[k, i] * result[k]
        result[i] = value
        out_ref[i : i + 1, :] = value


def exchanged(array, axis, first):
    peers = lax.axis_size(axis)
    order = [(first + i) % peers for i in range(peers)]
    return lax.all_to_all(array, axis, 0, 0, axis_index_groups=[order], tiled=True)


def on_device(
    attitude,
    slot_time,
    slot_parallax,
    slot_observed,
    slot_phase,
    slot_knot,
    block_source,
    block_count,
    prior,
):
    n_sky = lax.axis_size("sky")
    n_tm = lax.axis_size("tm")
    shard = attitude[:, 0, :]
    blocks = block_source.shape[0]
    owned = prior.shape[1]
    table = exchanged(jnp.broadcast_to(shard[None], (n_sky, *shard.shape)), "sky", SKY_FIRST)

    def rows(array):
        return array.reshape(-1, LANES)

    f32 = jnp.float32
    slot_rows = (SLOTS * blocks // LANES, LANES)
    block_rows = (blocks // LANES, LANES)
    given = [
        pltpu.with_memory_space_constraint(rows(array), pltpu.HBM)
        for array in (
            slot_phase, slot_knot, block_source, block_count, slot_time, slot_parallax, slot_observed,
        )
    ]
    octet, weight, extra, low, high = pl.pallas_call(
        prepare_kernel,
        out_shape=(
            jax.ShapeDtypeStruct((SLOTS, blocks), f32),
            jax.ShapeDtypeStruct((SLOTS, 8 * PAIRS, blocks), f32),
            jax.ShapeDtypeStruct((3, SLOTS, blocks), f32),
            jax.ShapeDtypeStruct((owned, blocks), f32),
            jax.ShapeDtypeStruct((n_tm, blocks), f32),
        ),
        in_specs=[pl.BlockSpec(memory_space=pltpu.HBM)] * 7,
        scratch_shapes=[
            pltpu.VMEM(slot_rows, f32),
            pltpu.VMEM(slot_rows, jnp.int32),
            pltpu.VMEM(block_rows, jnp.int32),
            pltpu.VMEM(block_rows, jnp.int32),
            pltpu.VMEM(slot_rows, f32),
            pltpu.VMEM(slot_rows, f32),
            pltpu.VMEM(slot_rows, f32),
            pltpu.SemaphoreType.DMA((7,)),
        ],
        cost_estimate=pl.CostEstimate(flops=0, bytes_accessed=8000000, transcendentals=0),
        compiler_params=pltpu.CompilerParams(vmem_limit_bytes=16 << 20),
        name="prepare",
    )(*given)
    partial = pl.pallas_call(
        sums_kernel,
        out_shape=jax.ShapeDtypeStruct((n_tm, 1, 20 * owned), f32),
        scratch_shapes=[pltpu.VMEM((COMPS, SLOTS, blocks), f32)],
        compiler_params=pltpu.CompilerParams(vmem_limit_bytes=16 << 20),
        name="sums",
    )(table, octet, weight, extra, low, high)
    parts = exchanged(partial, "tm", TM_FIRST)
    return pl.pallas_call(
        solve_kernel,
        out_shape=jax.ShapeDtypeStruct((5, owned), f32),
        compiler_params=pltpu.CompilerParams(vmem_limit_bytes=1 << 20),
        name="solve",
    )(parts, prior)


def solution(mesh):
    in_specs = (
        P(None, "tm", "sky"),
        P(("sky", "tm")),
        P(("sky", "tm")),
        P(("sky", "tm")),
        P(("sky", "tm")),
        P(("sky", "tm")),
        P(("sky", "tm")),
        P(("sky", "tm")),
        P(None, ("sky", "tm")),
    )
    out_specs = P(None, ("sky", "tm"))
    return jax.shard_map(
        on_device, mesh=mesh, in_specs=in_specs, out_specs=out_specs, check_vma=False
    )
```

```python
import jax
import jax.numpy as jnp
from jax import lax
from jax.experimental import pallas as pl
from jax.experimental.pallas import tpu as pltpu
from jax.sharding import PartitionSpec as P

PAIR_LIST = [(i, j) for i in range(5) for j in range(i, 5)]
LANES = 128
SLOTS = 32
COMPS = 4
PAIRS = 6
SKY_ORDER = [(13 + i) % 16 for i in range(16)]
TM_ORDER = [(22 + i) % 32 for i in range(32)]


def to_slot_rows(tile):
    turned = tile.T
    groups = LANES // SLOTS
    return jnp.concatenate([turned[g * SLOTS : (g + 1) * SLOTS] for g in range(groups)], axis=1)


def prepare_kernel(
    phase_in, knot_in, source_in, count_in, time_in, parallax_in, observed_in,
    octet_ref, weight_ref, extra_ref, low_ref, high_ref,
    phase_ref, knot_ref, source_ref, count_ref, time_ref, parallax_ref, observed_ref, sems,
):
    pairs = (
        (count_in, count_ref), (source_in, source_ref), (phase_in, phase_ref), (knot_in, knot_ref),
        (time_in, time_ref), (parallax_in, parallax_ref), (observed_in, observed_ref),
    )
    copies = [pltpu.make_async_copy(a, b, sems.at[i]) for i, (a, b) in enumerate(pairs)]
    for copy in copies:
        copy.start()
    for copy in copies:
        copy.wait()
    blocks = octet_ref.shape[1]
    groups = LANES // SLOTS
    per_group = blocks // groups
    row = lax.broadcasted_iota(jnp.int32, (blocks, blocks), 0)
    column = lax.broadcasted_iota(jnp.int32, (blocks, blocks), 1)
    moved = (row == groups * (column % per_group) + column // per_group).astype(jnp.bfloat16)

    def in_order(ref):
        natural = jnp.concatenate([ref[i : i + 1] for i in range(blocks // LANES)], axis=1)
        natural = jnp.broadcast_to(natural.astype(jnp.float32), (8, blocks)).astype(jnp.bfloat16)
        ordered = jnp.dot(natural, moved, preferred_element_type=jnp.float32)
        return (ordered + 0.5).astype(jnp.int32)

    count = in_order(count_ref)[:1]
    source = in_order(source_ref)[:1]
    slot = lax.broadcasted_iota(jnp.int32, (SLOTS, blocks), 0)
    live = (slot < count).astype(jnp.float32)
    extra_ref[0] = to_slot_rows(time_ref[...])
    extra_ref[1] = to_slot_rows(parallax_ref[...]) * live
    extra_ref[2] = to_slot_rows(observed_ref[...])
    owned = low_ref.shape[0]
    within = lax.broadcasted_iota(jnp.int32, low_ref.shape, 0)
    low_ref[...] = (source % owned == within).astype(jnp.float32)
    owner = source // owned
    for i, member in enumerate(TM_ORDER):
        high_ref[i : i + 1, :] = (owner == member).astype(jnp.float32)

    u = to_slot_rows(phase_ref[...])
    v = 1.0 - u
    weights = [
        live * (v * v * v / 6.0),
        live * ((3.0 * u * u * u - 6.0 * u * u + 4.0) / 6.0),
        live * ((-3.0 * u * u * u + 3.0 * u * u + 3.0 * u + 1.0) / 6.0),
        live * (u * u * u / 6.0),
    ]
    knot = to_slot_rows(knot_ref[...])
    start = knot & 7
    octet_ref[...] = (knot >> 3).astype(jnp.float32)
    later = lax.broadcasted_iota(jnp.int32, (8, blocks), 0) // COMPS
    for s in range(SLOTS):
        ahead = later - start[s : s + 1]
        for a in range(PAIRS):
            value = jnp.zeros((8, blocks), jnp.float32)
            for i in range(4):
                value = jnp.where(ahead == i - 2 * a, weights[i][s : s + 1], value)
            weight_ref[s, 8 * a : 8 * a + 8] = value


def octet_rows(table_ref):
    parts = table_ref.shape[0]
    lane = lax.broadcasted_iota(jnp.int32, (8, LANES), 1)
    sub = lax.broadcasted_iota(jnp.int32, (8, LANES), 0)
    pairs = [
        jnp.concatenate([table_ref[SKY_ORDER.index(2 * v + p)] for p in range(2)], axis=0)
        for v in range(parts // 2)
    ]
    in_place = (lane // 16) % 2 == sub // COMPS
    halves = []
    for h in range(2):
        wide = []
        for j in range(8):
            spot = 8 * (lane % 16) + j
            found = [
                jnp.take_along_axis(pairs[4 * h + q], spot, axis=1, mode="promise_in_bounds")
                for q in range(4)
            ]
            chosen = found[0]
            for q in range(1, 4):
                chosen = jnp.where(lane // 32 == q, found[q], chosen)
            wide.append(jnp.where(in_place, chosen, pltpu.roll(chosen, COMPS, 0)))
        halves.append([jnp.where(sub < COMPS, wide[2 * a], wide[2 * a + 1]) for a in range(4)])
    rows = []
    for a in range(4):
        rows.append(jnp.concatenate([halves[0][a], halves[1][a]], axis=1))
    for a in range(2):
        moved = [pltpu.roll(halves[h][a], LANES - 1, 1) for h in range(2)]
        rows.append(
            jnp.concatenate(
                [jnp.where(lane == LANES - 1, moved[1 - h], moved[h]) for h in range(2)], axis=1
            )
        )
    return jnp.concatenate(rows, axis=0)


def in_three(array):
    pieces = []
    for _ in range(3):
        pieces.append(array.astype(jnp.bfloat16))
        array = array - pieces[-1].astype(jnp.float32)
    return pieces


def sums_kernel(
    table_ref, octet_ref, weight_ref, extra_ref, low_ref, high_ref,
    out_ref, quat_ref,
):
    blocks = octet_ref.shape[1]
    high_rows = 8 * PAIRS
    table = jnp.concatenate(in_three(octet_rows(table_ref)), axis=0)
    octets = table.shape[1]
    numbers = lax.broadcasted_iota(jnp.int32, (octets, blocks), 0).astype(jnp.float32).astype(jnp.bfloat16)
    one, zero = jnp.bfloat16(1.0), jnp.bfloat16(0.0)
    for s in range(SLOTS):
        here = jnp.broadcast_to(octet_ref[s : s + 1, :], (16, blocks)).astype(jnp.bfloat16)
        here = jnp.concatenate([here] * (octets // 16), axis=0)
        pick = jnp.where(numbers == here, one, zero)
        got = jnp.dot(table, pick, preferred_element_type=jnp.float32)
        got = got[:high_rows] + got[high_rows : 2 * high_rows] + got[2 * high_rows :]
        got = got * weight_ref[s]
        both = got[:8]
        for a in range(1, PAIRS):
            both = both + got[8 * a : 8 * a + 8]
        both = both + pltpu.roll(both, COMPS, 0)
        for m in range(COMPS):
            quat_ref[m, s : s + 1, :] = both[m : m + 1]

    totals = [None] * 20
    for at in range(SLOTS // 8):
        here = slice(8 * at, 8 * at + 8)
        q0, q1, q2, q3 = (quat_ref[m, here, :] for m in range(COMPS))
        cross = q0 * q0 + q1 * q1 - q2 * q2 - q3 * q3
        along = 2.0 * (q1 * q2 + q0 * q3)
        tilt = 2.0 * (q1 * q3 - q0 * q2)
        time = extra_ref[0, here, :]
        design = [cross, along, extra_ref[1, here, :], time * cross, time * along]
        residual = extra_ref[2, here, :] - tilt
        products = [design[i] * design[j] for i, j in PAIR_LIST]
        products += [design[i] * residual for i in range(5)]
        totals = [p if t is None else t + p for t, p in zip(totals, products)]

    low = low_ref[...]
    spread = jnp.concatenate([jnp.sum(t, axis=0, keepdims=True) * low for t in totals], axis=0)
    high = high_ref[...].astype(jnp.bfloat16)
    result = None
    for piece in in_three(spread):
        got = lax.dot_general(
            high, piece, (((1,), (1,)), ((), ())), preferred_element_type=jnp.float32
        )
        result = got if result is None else result + got
    for j in range(out_ref.shape[0]):
        out_ref[j] = result[j : j + 1]


def solve_kernel(parts_ref, prior_ref, out_ref):
    owned = prior_ref.shape[1]
    total = jnp.sum(parts_ref[...], axis=0)
    total = jnp.broadcast_to(total, (8, total.shape[1]))
    tiles = [total[:, :LANES], jnp.concatenate([total[:, LANES:], total[:, : 2 * LANES - total.shape[1]]], axis=1)]
    normal = []
    for p in range(20):
        tile, lane = divmod(owned * p, LANES)
        normal.append(pltpu.roll(tiles[tile], LANES - lane, 1) if lane else tiles[tile])
    entry = {}
    for index, (i, j) in enumerate(PAIR_LIST):
        entry[j, i] = normal[index]
    for i in range(5):
        own = jnp.broadcast_to(prior_ref[i : i + 1, :], (8, owned))
        entry[i, i] = entry[i, i] + jnp.concatenate([own] * (LANES // owned), axis=1)
    right = normal[15:]
    lower = {}
    inverse = []
    for col in range(5):
        inverse.append(1.0 / entry[col, col])
        for row in range(col + 1, 5):
            lower[row, col] = entry[row, col] * inverse[col]
        for row in range(col + 1, 5):
            for other in range(col + 1, row + 1):
                entry[row, other] = entry[row, other] - lower[row, col] * entry[other, col]
            right[row] = right[row] - lower[row, col] * right[col]
    result = [None] * 5
    for i in range(4, -1, -1):
        value = right[i] * inverse[i]
        for k in range(i + 1, 5):
            value = value - lower[k, i] * result[k]
        result[i] = value
        out_ref[i : i + 1, :] = value[:1, :owned]


def exchanged(array, axis, order):
    return lax.all_to_all(array, axis, 0, 0, axis_index_groups=[order], tiled=True)


def on_device(
    attitude,
    slot_time,
    slot_parallax,
    slot_observed,
    slot_phase,
    slot_knot,
    block_source,
    block_count,
    prior,
):
    n_sky = lax.axis_size("sky")
    n_tm = lax.axis_size("tm")
    shard = attitude[:, 0, :]
    blocks = block_source.shape[0]
    owned = prior.shape[1]
    table = exchanged(jnp.broadcast_to(shard[None], (n_sky, *shard.shape)), "sky", SKY_ORDER)

    def rows(array):
        return array.reshape(-1, LANES)

    f32 = jnp.float32
    slot_rows = (SLOTS * blocks // LANES, LANES)
    block_rows = (blocks // LANES, LANES)
    given = [
        pltpu.with_memory_space_constraint(rows(array), pltpu.HBM)
        for array in (
            slot_phase, slot_knot, block_source, block_count, slot_time, slot_parallax, slot_observed,
        )
    ]
    octet, weight, extra, low, high = pl.pallas_call(
        prepare_kernel,
        out_shape=(
            jax.ShapeDtypeStruct((SLOTS, blocks), f32),
            jax.ShapeDtypeStruct((SLOTS, 8 * PAIRS, blocks), f32),
            jax.ShapeDtypeStruct((3, SLOTS, blocks), f32),
            jax.ShapeDtypeStruct((owned, blocks), f32),
            jax.ShapeDtypeStruct((n_tm, blocks), f32),
        ),
        in_specs=[pl.BlockSpec(memory_space=pltpu.HBM)] * 7,
        scratch_shapes=[
            pltpu.VMEM(slot_rows, f32),
            pltpu.VMEM(slot_rows, jnp.int32),
            pltpu.VMEM(block_rows, jnp.int32),
            pltpu.VMEM(block_rows, jnp.int32),
            pltpu.VMEM(slot_rows, f32),
            pltpu.VMEM(slot_rows, f32),
            pltpu.VMEM(slot_rows, f32),
            pltpu.SemaphoreType.DMA((7,)),
        ],
        cost_estimate=pl.CostEstimate(flops=0, bytes_accessed=8000000, transcendentals=0),
        compiler_params=pltpu.CompilerParams(vmem_limit_bytes=16 << 20),
        name="prepare",
    )(*given)
    partial = pl.pallas_call(
        sums_kernel,
        out_shape=jax.ShapeDtypeStruct((n_tm, 1, 20 * owned), f32),
        scratch_shapes=[pltpu.VMEM((COMPS, SLOTS, blocks), f32)],
        compiler_params=pltpu.CompilerParams(vmem_limit_bytes=16 << 20),
        name="sums",
    )(table, octet, weight, extra, low, high)
    parts = exchanged(partial, "tm", TM_ORDER)
    return pl.pallas_call(
        solve_kernel,
        out_shape=jax.ShapeDtypeStruct((5, owned), f32),
        compiler_params=pltpu.CompilerParams(vmem_limit_bytes=1 << 20),
        name="solve",
    )(parts, prior)


def solution(mesh):
    in_specs = (
        P(None, "tm", "sky"),
        P(("sky", "tm")),
        P(("sky", "tm")),
        P(("sky", "tm")),
        P(("sky", "tm")),
        P(("sky", "tm")),
        P(("sky", "tm")),
        P(("sky", "tm")),
        P(None, ("sky", "tm")),
    )
    out_specs = P(None, ("sky", "tm"))
    return jax.shard_map(
        on_device, mesh=mesh, in_specs=in_specs, out_specs=out_specs, check_vma=False
    )
```

```python
import jax
import jax.numpy as jnp
from jax import lax
from jax.experimental import pallas as pl
from jax.experimental.pallas import tpu as pltpu
from jax.sharding import PartitionSpec as P

PAIR_LIST = [(i, j) for i in range(5) for j in range(i, 5)]
LANES = 128
SLOTS = 32
COMPS = 4
PAIRS = 6
SKY_ORDER = [(13 + i) % 16 for i in range(16)]
TM_ORDER = [(22 + i) % 32 for i in range(32)]


def to_slot_rows(tile):
    turned = tile.T
    groups = LANES // SLOTS
    return jnp.concatenate([turned[g * SLOTS : (g + 1) * SLOTS] for g in range(groups)], axis=1)


def fetch_kernel(shard_in, *refs):
    count = (len(refs) - 3) // 2
    given, (copies_ref, *here, shard_ref, sems) = refs[:count], refs[count:]
    first = pltpu.make_async_copy(shard_in, shard_ref, sems.at[count])
    first.start()
    others = [pltpu.make_async_copy(x, y, sems.at[i]) for i, (x, y) in enumerate(zip(given, here))]
    for copy in others:
        copy.start()
    first.wait()
    shard = shard_ref[:, 0, :]
    for i in range(copies_ref.shape[0]):
        copies_ref[i] = shard
    for copy in others:
        copy.wait()


def octet_rows(table_ref):
    parts = table_ref.shape[0]
    lane = lax.broadcasted_iota(jnp.int32, (8, LANES), 1)
    sub = lax.broadcasted_iota(jnp.int32, (8, LANES), 0)
    pairs = [
        jnp.concatenate([table_ref[SKY_ORDER.index(2 * v + p)] for p in range(2)], axis=0)
        for v in range(parts // 2)
    ]
    in_place = (lane // 16) % 2 == sub // COMPS
    halves = []
    for h in range(2):
        wide = []
        for j in range(8):
            spot = 8 * (lane % 16) + j
            found = [
                jnp.take_along_axis(pairs[4 * h + q], spot, axis=1, mode="promise_in_bounds")
                for q in range(4)
            ]
            chosen = found[0]
            for q in range(1, 4):
                chosen = jnp.where(lane // 32 == q, found[q], chosen)
            wide.append(jnp.where(in_place, chosen, pltpu.roll(chosen, COMPS, 0)))
        halves.append([jnp.where(sub < COMPS, wide[2 * a], wide[2 * a + 1]) for a in range(4)])
    rows = []
    for a in range(4):
        rows.append(jnp.concatenate([halves[0][a], halves[1][a]], axis=1))
    for a in range(2):
        moved = [pltpu.roll(halves[h][a], LANES - 1, 1) for h in range(2)]
        rows.append(
            jnp.concatenate(
                [jnp.where(lane == LANES - 1, moved[1 - h], moved[h]) for h in range(2)], axis=1
            )
        )
    return jnp.concatenate(rows, axis=0)


def in_three(array):
    pieces = []
    for _ in range(3):
        pieces.append(array.astype(jnp.bfloat16))
        array = array - pieces[-1].astype(jnp.float32)
    return pieces


def sums_kernel(
    table_ref, phase_ref, knot_ref, source_ref, count_ref, time_ref, parallax_ref, observed_ref,
    out_ref, quat_ref,
):
    owners, owned = out_ref.shape[0], out_ref.shape[2] // 20
    blocks = quat_ref.shape[2]
    groups = LANES // SLOTS
    per_group = blocks // groups
    row = lax.broadcasted_iota(jnp.int32, (blocks, blocks), 0)
    column = lax.broadcasted_iota(jnp.int32, (blocks, blocks), 1)
    moved = (row == groups * (column % per_group) + column // per_group).astype(jnp.bfloat16)

    def in_order(ref):
        natural = jnp.concatenate([ref[i : i + 1] for i in range(blocks // LANES)], axis=1)
        natural = jnp.broadcast_to(natural.astype(jnp.float32), (8, blocks)).astype(jnp.bfloat16)
        ordered = jnp.dot(natural, moved, preferred_element_type=jnp.float32)
        return (ordered + 0.5).astype(jnp.int32)

    u = to_slot_rows(phase_ref[...])
    v = 1.0 - u
    weights = [
        v * v * v / 6.0,
        (3.0 * u * u * u - 6.0 * u * u + 4.0) / 6.0,
        (-3.0 * u * u * u + 3.0 * u * u + 3.0 * u + 1.0) / 6.0,
        u * u * u / 6.0,
    ]
    knot = to_slot_rows(knot_ref[...])
    start = knot & 7
    octet = (knot >> 3).astype(jnp.float32)
    later = lax.broadcasted_iota(jnp.int32, (8, blocks), 0) // COMPS
    high_rows = 8 * PAIRS
    table = jnp.concatenate(in_three(octet_rows(table_ref)), axis=0)
    octets = table.shape[1]
    numbers = lax.broadcasted_iota(jnp.int32, (octets, blocks), 0).astype(jnp.float32).astype(jnp.bfloat16)
    one, zero = jnp.bfloat16(1.0), jnp.bfloat16(0.0)
    for s in range(SLOTS):
        here = jnp.broadcast_to(octet[s : s + 1], (16, blocks)).astype(jnp.bfloat16)
        here = jnp.concatenate([here] * (octets // 16), axis=0)
        pick = jnp.where(numbers == here, one, zero)
        got = jnp.dot(table, pick, preferred_element_type=jnp.float32)
        got = got[:high_rows] + got[high_rows : 2 * high_rows] + got[2 * high_rows :]
        ahead = later - start[s : s + 1]
        both = None
        for a in range(PAIRS):
            value = jnp.zeros((8, blocks), jnp.float32)
            for i in range(4):
                value = jnp.where(ahead == i - 2 * a, weights[i][s : s + 1], value)
            term = value * got[8 * a : 8 * a + 8]
            both = term if both is None else both + term
        both = both + pltpu.roll(both, COMPS, 0)
        for m in range(COMPS):
            quat_ref[m, s : s + 1, :] = both[m : m + 1]

    count = in_order(count_ref)[:1]
    source = in_order(source_ref)[:1]
    slot = lax.broadcasted_iota(jnp.int32, (SLOTS, blocks), 0)
    live = (slot < count).astype(jnp.float32)
    times = to_slot_rows(time_ref[...])
    parallaxes = to_slot_rows(parallax_ref[...]) * live
    observations = to_slot_rows(observed_ref[...])
    totals = [None] * 20
    for at in range(SLOTS // 8):
        here = slice(8 * at, 8 * at + 8)
        q0, q1, q2, q3 = (quat_ref[m, here, :] for m in range(COMPS))
        cross = live[here] * (q0 * q0 + q1 * q1 - q2 * q2 - q3 * q3)
        along = live[here] * (2.0 * (q1 * q2 + q0 * q3))
        tilt = 2.0 * (q1 * q3 - q0 * q2)
        time = times[here]
        design = [cross, along, parallaxes[here], time * cross, time * along]
        residual = observations[here] - tilt
        products = [design[i] * design[j] for i, j in PAIR_LIST]
        products += [design[i] * residual for i in range(5)]
        totals = [p if t is None else t + p for t, p in zip(totals, products)]

    within = lax.broadcasted_iota(jnp.int32, (owned, blocks), 0)
    low = (source % owned == within).astype(jnp.float32)
    spread = jnp.concatenate([jnp.sum(t, axis=0, keepdims=True) * low for t in totals], axis=0)
    owner = (lax.broadcasted_iota(jnp.int32, (owners, blocks), 0) + TM_ORDER[0]) % owners
    high = (source // owned == owner).astype(jnp.float32).astype(jnp.bfloat16)
    result = None
    for piece in in_three(spread):
        got = lax.dot_general(
            high, piece, (((1,), (1,)), ((), ())), preferred_element_type=jnp.float32
        )
        result = got if result is None else result + got
    for j in range(out_ref.shape[0]):
        out_ref[j] = result[j : j + 1]


def solve_kernel(parts_ref, prior_ref, out_ref):
    owned = prior_ref.shape[1]
    total = jnp.sum(parts_ref[...], axis=0)
    total = jnp.broadcast_to(total, (8, total.shape[1]))
    tiles = [total[:, :LANES], jnp.concatenate([total[:, LANES:], total[:, : 2 * LANES - total.shape[1]]], axis=1)]
    normal = []
    for p in range(20):
        tile, lane = divmod(owned * p, LANES)
        normal.append(pltpu.roll(tiles[tile], LANES - lane, 1) if lane else tiles[tile])
    entry = {}
    for index, (i, j) in enumerate(PAIR_LIST):
        entry[j, i] = normal[index]
    for i in range(5):
        own = jnp.broadcast_to(prior_ref[i : i + 1, :], (8, owned))
        entry[i, i] = entry[i, i] + jnp.concatenate([own] * (LANES // owned), axis=1)
    right = normal[15:]
    lower = {}
    inverse = []
    for col in range(5):
        inverse.append(1.0 / entry[col, col])
        for row in range(col + 1, 5):
            lower[row, col] = entry[row, col] * inverse[col]
        for row in range(col + 1, 5):
            for other in range(col + 1, row + 1):
                entry[row, other] = entry[row, other] - lower[row, col] * entry[other, col]
            right[row] = right[row] - lower[row, col] * right[col]
    result = [None] * 5
    for i in range(4, -1, -1):
        value = right[i] * inverse[i]
        for k in range(i + 1, 5):
            value = value - lower[k, i] * result[k]
        result[i] = value
        out_ref[i : i + 1, :] = value[:1, :owned]


def exchanged(array, axis, order):
    return lax.all_to_all(array, axis, 0, 0, axis_index_groups=[order], tiled=True)


def on_device(
    attitude,
    slot_time,
    slot_parallax,
    slot_observed,
    slot_phase,
    slot_knot,
    block_source,
    block_count,
    prior,
):
    n_sky = lax.axis_size("sky")
    n_tm = lax.axis_size("tm")
    shard = attitude[:, 0, :]
    blocks = block_source.shape[0]
    owned = prior.shape[1]
    f32 = jnp.float32

    def rows(array):
        return array.reshape(-1, LANES)

    given = [attitude] + [
        rows(array)
        for array in (
            slot_phase, slot_knot, block_source, block_count, slot_time, slot_parallax, slot_observed,
        )
    ]
    copies, *here = pl.pallas_call(
        fetch_kernel,
        out_shape=[jax.ShapeDtypeStruct((n_sky, *shard.shape), f32)]
        + [jax.ShapeDtypeStruct(array.shape, array.dtype) for array in given[1:]],
        in_specs=[pl.BlockSpec(memory_space=pltpu.HBM)] * len(given),
        scratch_shapes=[pltpu.VMEM(attitude.shape, f32), pltpu.SemaphoreType.DMA((len(given),))],
        compiler_params=pltpu.CompilerParams(vmem_limit_bytes=4 << 20),
        name="fetch",
    )(*[pltpu.with_memory_space_constraint(array, pltpu.HBM) for array in given])
    table = exchanged(copies, "sky", SKY_ORDER)
    partial = pl.pallas_call(
        sums_kernel,
        out_shape=jax.ShapeDtypeStruct((n_tm, 1, 20 * owned), f32),
        scratch_shapes=[pltpu.VMEM((COMPS, SLOTS, blocks), f32)],
        compiler_params=pltpu.CompilerParams(vmem_limit_bytes=16 << 20),
        name="sums",
    )(table, *here)
    parts = exchanged(partial, "tm", TM_ORDER)
    return pl.pallas_call(
        solve_kernel,
        out_shape=jax.ShapeDtypeStruct((5, owned), f32),
        compiler_params=pltpu.CompilerParams(vmem_limit_bytes=1 << 20),
        name="solve",
    )(parts, prior)


def solution(mesh):
    in_specs = (
        P(None, "tm", "sky"),
        P(("sky", "tm")),
        P(("sky", "tm")),
        P(("sky", "tm")),
        P(("sky", "tm")),
        P(("sky", "tm")),
        P(("sky", "tm")),
        P(("sky", "tm")),
        P(None, ("sky", "tm")),
    )
    out_specs = P(None, ("sky", "tm"))
    return jax.shard_map(
        on_device, mesh=mesh, in_specs=in_specs, out_specs=out_specs, check_vma=False
    )
```

```python
import jax
import jax.numpy as jnp
from jax import lax
from jax.experimental import pallas as pl
from jax.experimental.pallas import tpu as pltpu
from jax.sharding import PartitionSpec as P

PAIR_LIST = [(i, j) for i in range(5) for j in range(i, 5)]
LANES = 128
SLOTS = 32
COMPS = 4
PAIRS = 6
SKY_ORDER = [(13 + i) % 16 for i in range(16)]
TM_ORDER = [(22 + i) % 32 for i in range(32)]


def to_slot_rows(tile):
    turned = tile.T
    groups = LANES // SLOTS
    return jnp.concatenate([turned[g * SLOTS : (g + 1) * SLOTS] for g in range(groups)], axis=1)


def fetch_kernel(shard_in, *refs):
    count = (len(refs) - 3) // 2
    given, (copies_ref, *here, shard_ref, sems) = refs[:count], refs[count:]
    first = pltpu.make_async_copy(shard_in, shard_ref, sems.at[count])
    first.start()
    others = [pltpu.make_async_copy(x, y, sems.at[i]) for i, (x, y) in enumerate(zip(given, here))]
    for copy in others:
        copy.start()
    first.wait()
    shard = shard_ref[:, 0, :]
    for i in range(copies_ref.shape[0]):
        copies_ref[i] = shard
    for copy in others:
        copy.wait()


def octet_rows(table_ref):
    parts = table_ref.shape[0]
    lane = lax.broadcasted_iota(jnp.int32, (8, LANES), 1)
    sub = lax.broadcasted_iota(jnp.int32, (8, LANES), 0)
    pairs = [
        jnp.concatenate([table_ref[SKY_ORDER.index(2 * v + p)] for p in range(2)], axis=0)
        for v in range(parts // 2)
    ]
    in_place = (lane // 16) % 2 == sub // COMPS
    halves = []
    for h in range(2):
        wide = []
        for j in range(8):
            spot = 8 * (lane % 16) + j
            found = [
                jnp.take_along_axis(pairs[4 * h + q], spot, axis=1, mode="promise_in_bounds")
                for q in range(4)
            ]
            chosen = found[0]
            for q in range(1, 4):
                chosen = jnp.where(lane // 32 == q, found[q], chosen)
            wide.append(jnp.where(in_place, chosen, pltpu.roll(chosen, COMPS, 0)))
        halves.append([jnp.where(sub < COMPS, wide[2 * a], wide[2 * a + 1]) for a in range(4)])
    rows = []
    for a in range(4):
        rows.append(jnp.concatenate([halves[0][a], halves[1][a]], axis=1))
    for a in range(2):
        moved = [pltpu.roll(halves[h][a], LANES - 1, 1) for h in range(2)]
        rows.append(
            jnp.concatenate(
                [jnp.where(lane == LANES - 1, moved[1 - h], moved[h]) for h in range(2)], axis=1
            )
        )
    return jnp.concatenate(rows, axis=0)


def in_three(array):
    pieces = []
    for _ in range(3):
        pieces.append(array.astype(jnp.bfloat16))
        array = array - pieces[-1].astype(jnp.float32)
    return pieces


def sums_kernel(
    table_ref, phase_ref, knot_ref, source_ref, count_ref, time_ref, parallax_ref, observed_ref,
    out_ref, quat_ref,
):
    owners, owned = out_ref.shape[0], out_ref.shape[2] // 20
    blocks = quat_ref.shape[2]
    groups = LANES // SLOTS
    per_group = blocks // groups
    row = lax.broadcasted_iota(jnp.int32, (blocks, blocks), 0)
    column = lax.broadcasted_iota(jnp.int32, (blocks, blocks), 1)
    moved = (row == groups * (column % per_group) + column // per_group).astype(jnp.bfloat16)

    def in_order(ref):
        natural = jnp.concatenate([ref[i : i + 1] for i in range(blocks // LANES)], axis=1)
        natural = jnp.broadcast_to(natural.astype(jnp.float32), (8, blocks)).astype(jnp.bfloat16)
        ordered = jnp.dot(natural, moved, preferred_element_type=jnp.float32)
        return (ordered + 0.5).astype(jnp.int32)

    u = to_slot_rows(phase_ref[...])
    v = 1.0 - u
    weights = [
        v * v * v / 6.0,
        (3.0 * u * u * u - 6.0 * u * u + 4.0) / 6.0,
        (-3.0 * u * u * u + 3.0 * u * u + 3.0 * u + 1.0) / 6.0,
        u * u * u / 6.0,
    ]
    knot = to_slot_rows(knot_ref[...])
    start = knot & 7
    octet = (knot >> 3).astype(jnp.float32)
    odd, none = start & 1 != 0, jnp.zeros_like(u)
    placed = [
        jnp.where(odd, before, now)
        for before, now in zip([none] + weights + [none], weights + [none, none])
    ]
    first = lax.broadcasted_iota(jnp.int32, (8, blocks), 0) < COMPS
    high_rows = 8 * PAIRS
    table = jnp.concatenate(in_three(octet_rows(table_ref)), axis=0)
    octets = table.shape[1]
    numbers = lax.broadcasted_iota(jnp.int32, (octets, blocks), 0).astype(jnp.float32).astype(jnp.bfloat16)
    one, zero = jnp.bfloat16(1.0), jnp.bfloat16(0.0)
    for s in range(SLOTS):
        here = jnp.broadcast_to(octet[s : s + 1], (16, blocks)).astype(jnp.bfloat16)
        here = jnp.concatenate([here] * (octets // 16), axis=0)
        pick = jnp.where(numbers == here, one, zero)
        got = jnp.dot(table, pick, preferred_element_type=jnp.float32)
        got = got[:high_rows] + got[high_rows : 2 * high_rows] + got[2 * high_rows :]
        pairs = [got[8 * a : 8 * a + 8] for a in range(PAIRS)]
        by_four = jnp.broadcast_to(start[s : s + 1], (8, blocks)) & 4 != 0
        by_two = jnp.broadcast_to(start[s : s + 1], (8, blocks)) & 2 != 0
        pairs = [jnp.where(by_four, pairs[a + 2], pairs[a]) for a in range(4)]
        pairs = [jnp.where(by_two, pairs[a + 1], pairs[a]) for a in range(3)]
        both = None
        for a in range(3):
            value = jnp.where(first, placed[2 * a][s : s + 1], placed[2 * a + 1][s : s + 1])
            term = value * pairs[a]
            both = term if both is None else both + term
        both = both + pltpu.roll(both, COMPS, 0)
        for m in range(COMPS):
            quat_ref[m, s : s + 1, :] = both[m : m + 1]

    count = in_order(count_ref)[:1]
    source = in_order(source_ref)[:1]
    slot = lax.broadcasted_iota(jnp.int32, (SLOTS, blocks), 0)
    live = (slot < count).astype(jnp.float32)
    times = to_slot_rows(time_ref[...])
    parallaxes = to_slot_rows(parallax_ref[...]) * live
    observations = to_slot_rows(observed_ref[...])
    totals = [None] * 20
    for at in range(SLOTS // 8):
        here = slice(8 * at, 8 * at + 8)
        q0, q1, q2, q3 = (quat_ref[m, here, :] for m in range(COMPS))
        cross = live[here] * (q0 * q0 + q1 * q1 - q2 * q2 - q3 * q3)
        along = live[here] * (2.0 * (q1 * q2 + q0 * q3))
        tilt = 2.0 * (q1 * q3 - q0 * q2)
        time = times[here]
        design = [cross, along, parallaxes[here], time * cross, time * along]
        residual = observations[here] - tilt
        products = [design[i] * design[j] for i, j in PAIR_LIST]
        products += [design[i] * residual for i in range(5)]
        totals = [p if t is None else t + p for t, p in zip(totals, products)]

    within = lax.broadcasted_iota(jnp.int32, (owned, blocks), 0)
    low = (source % owned == within).astype(jnp.float32)
    spread = jnp.concatenate([jnp.sum(t, axis=0, keepdims=True) * low for t in totals], axis=0)
    owner = (lax.broadcasted_iota(jnp.int32, (owners, blocks), 0) + TM_ORDER[0]) % owners
    high = (source // owned == owner).astype(jnp.float32).astype(jnp.bfloat16)
    result = None
    for piece in in_three(spread):
        got = lax.dot_general(
            high, piece, (((1,), (1,)), ((), ())), preferred_element_type=jnp.float32
        )
        result = got if result is None else result + got
    for j in range(out_ref.shape[0]):
        out_ref[j] = result[j : j + 1]


def solve_kernel(parts_ref, prior_ref, out_ref):
    owned = prior_ref.shape[1]
    total = jnp.sum(parts_ref[...], axis=0)
    total = jnp.broadcast_to(total, (8, total.shape[1]))
    tiles = [total[:, :LANES], jnp.concatenate([total[:, LANES:], total[:, : 2 * LANES - total.shape[1]]], axis=1)]
    normal = []
    for p in range(20):
        tile, lane = divmod(owned * p, LANES)
        normal.append(pltpu.roll(tiles[tile], LANES - lane, 1) if lane else tiles[tile])
    entry = {}
    for index, (i, j) in enumerate(PAIR_LIST):
        entry[j, i] = normal[index]
    for i in range(5):
        own = jnp.broadcast_to(prior_ref[i : i + 1, :], (8, owned))
        entry[i, i] = entry[i, i] + jnp.concatenate([own] * (LANES // owned), axis=1)
    right = normal[15:]
    lower = {}
    inverse = []
    for col in range(5):
        inverse.append(1.0 / entry[col, col])
        for row in range(col + 1, 5):
            lower[row, col] = entry[row, col] * inverse[col]
        for row in range(col + 1, 5):
            for other in range(col + 1, row + 1):
                entry[row, other] = entry[row, other] - lower[row, col] * entry[other, col]
            right[row] = right[row] - lower[row, col] * right[col]
    result = [None] * 5
    for i in range(4, -1, -1):
        value = right[i] * inverse[i]
        for k in range(i + 1, 5):
            value = value - lower[k, i] * result[k]
        result[i] = value
        out_ref[i : i + 1, :] = value[:1, :owned]


def exchanged(array, axis, order):
    return lax.all_to_all(array, axis, 0, 0, axis_index_groups=[order], tiled=True)


def on_device(
    attitude,
    slot_time,
    slot_parallax,
    slot_observed,
    slot_phase,
    slot_knot,
    block_source,
    block_count,
    prior,
):
    n_sky = lax.axis_size("sky")
    n_tm = lax.axis_size("tm")
    shard = attitude[:, 0, :]
    blocks = block_source.shape[0]
    owned = prior.shape[1]
    f32 = jnp.float32

    def rows(array):
        return array.reshape(-1, LANES)

    given = [attitude] + [
        rows(array)
        for array in (
            slot_phase, slot_knot, block_source, block_count, slot_time, slot_parallax, slot_observed,
        )
    ]
    copies, *here = pl.pallas_call(
        fetch_kernel,
        out_shape=[jax.ShapeDtypeStruct((n_sky, *shard.shape), f32)]
        + [jax.ShapeDtypeStruct(array.shape, array.dtype) for array in given[1:]],
        in_specs=[pl.BlockSpec(memory_space=pltpu.HBM)] * len(given),
        scratch_shapes=[pltpu.VMEM(attitude.shape, f32), pltpu.SemaphoreType.DMA((len(given),))],
        compiler_params=pltpu.CompilerParams(vmem_limit_bytes=4 << 20),
        name="fetch",
    )(*[pltpu.with_memory_space_constraint(array, pltpu.HBM) for array in given])
    table = exchanged(copies, "sky", SKY_ORDER)
    partial = pl.pallas_call(
        sums_kernel,
        out_shape=jax.ShapeDtypeStruct((n_tm, 1, 20 * owned), f32),
        scratch_shapes=[pltpu.VMEM((COMPS, SLOTS, blocks), f32)],
        compiler_params=pltpu.CompilerParams(vmem_limit_bytes=16 << 20),
        name="sums",
    )(table, *here)
    parts = exchanged(partial, "tm", TM_ORDER)
    return pl.pallas_call(
        solve_kernel,
        out_shape=jax.ShapeDtypeStruct((5, owned), f32),
        compiler_params=pltpu.CompilerParams(vmem_limit_bytes=1 << 20),
        name="solve",
    )(parts, prior)


def solution(mesh):
    in_specs = (
        P(None, "tm", "sky"),
        P(("sky", "tm")),
        P(("sky", "tm")),
        P(("sky", "tm")),
        P(("sky", "tm")),
        P(("sky", "tm")),
        P(("sky", "tm")),
        P(("sky", "tm")),
        P(None, ("sky", "tm")),
    )
    out_specs = P(None, ("sky", "tm"))
    return jax.shard_map(
        on_device, mesh=mesh, in_specs=in_specs, out_specs=out_specs, check_vma=False
    )
```

```python
import jax
import jax.numpy as jnp
from jax import lax
from jax.experimental import pallas as pl
from jax.experimental.pallas import tpu as pltpu
from jax.sharding import PartitionSpec as P

PAIR_LIST = [(i, j) for i in range(5) for j in range(i, 5)]
LANES = 128
SLOTS = 32
COMPS = 4
PAIRS = 6
SKY_ORDER = [(13 + i) % 16 for i in range(16)]
TM_ORDER = [(22 + i) % 32 for i in range(32)]


def to_slot_rows(tile):
    turned = tile.T
    groups = LANES // SLOTS
    return jnp.concatenate([turned[g * SLOTS : (g + 1) * SLOTS] for g in range(groups)], axis=1)


def fetch_kernel(shard_in, *refs):
    count = (len(refs) - 3) // 2
    given, (copies_ref, *here, shard_ref, sems) = refs[:count], refs[count:]
    first = pltpu.make_async_copy(shard_in, shard_ref, sems.at[count])
    first.start()
    others = [pltpu.make_async_copy(x, y, sems.at[i]) for i, (x, y) in enumerate(zip(given, here))]
    for copy in others:
        copy.start()
    first.wait()
    shard = shard_ref[:, 0, :]
    for i in range(copies_ref.shape[0]):
        copies_ref[i] = shard
    for copy in others:
        copy.wait()


def octet_rows(table_ref):
    parts = table_ref.shape[0]
    lane = lax.broadcasted_iota(jnp.int32, (8, LANES), 1)
    sub = lax.broadcasted_iota(jnp.int32, (8, LANES), 0)
    pairs = [
        jnp.concatenate([table_ref[SKY_ORDER.index(2 * v + p)] for p in range(2)], axis=0)
        for v in range(parts // 2)
    ]
    in_place = (lane // 16) % 2 == sub // COMPS
    halves = []
    for h in range(2):
        wide = []
        for j in range(8):
            spot = 8 * (lane % 16) + j
            found = [
                jnp.take_along_axis(pairs[4 * h + q], spot, axis=1, mode="promise_in_bounds")
                for q in range(4)
            ]
            chosen = found[0]
            for q in range(1, 4):
                chosen = jnp.where(lane // 32 == q, found[q], chosen)
            wide.append(jnp.where(in_place, chosen, pltpu.roll(chosen, COMPS, 0)))
        halves.append([jnp.where(sub < COMPS, wide[2 * a], wide[2 * a + 1]) for a in range(4)])
    rows = []
    for a in range(4):
        rows.append(jnp.concatenate([halves[0][a], halves[1][a]], axis=1))
    for a in range(2):
        moved = [pltpu.roll(halves[h][a], LANES - 1, 1) for h in range(2)]
        rows.append(
            jnp.concatenate(
                [jnp.where(lane == LANES - 1, moved[1 - h], moved[h]) for h in range(2)], axis=1
            )
        )
    return jnp.concatenate(rows, axis=0)


def in_three(array):
    pieces = []
    for _ in range(3):
        pieces.append(array.astype(jnp.bfloat16))
        array = array - pieces[-1].astype(jnp.float32)
    return pieces


def sums_kernel(
    table_ref, phase_ref, knot_ref, source_ref, count_ref, time_ref, parallax_ref, observed_ref,
    out_ref, quat_ref,
):
    owners, owned = out_ref.shape[0], out_ref.shape[2] // 20
    blocks = quat_ref.shape[2]
    groups = LANES // SLOTS
    per_group = blocks // groups
    row = lax.broadcasted_iota(jnp.int32, (blocks, blocks), 0)
    column = lax.broadcasted_iota(jnp.int32, (blocks, blocks), 1)
    moved = (row == groups * (column % per_group) + column // per_group).astype(jnp.bfloat16)

    def in_order(ref):
        natural = jnp.concatenate([ref[i : i + 1] for i in range(blocks // LANES)], axis=1)
        natural = jnp.broadcast_to(natural.astype(jnp.float32), (8, blocks)).astype(jnp.bfloat16)
        ordered = jnp.dot(natural, moved, preferred_element_type=jnp.float32)
        return (ordered + 0.5).astype(jnp.int32)

    u = to_slot_rows(phase_ref[...])
    v = 1.0 - u
    weights = [
        v * v * v / 6.0,
        (3.0 * u * u * u - 6.0 * u * u + 4.0) / 6.0,
        (-3.0 * u * u * u + 3.0 * u * u + 3.0 * u + 1.0) / 6.0,
        u * u * u / 6.0,
    ]
    knot = to_slot_rows(knot_ref[...])
    start = knot & 7
    octet = (knot >> 3).astype(jnp.float32)
    odd, none = start & 1 != 0, jnp.zeros_like(u)
    placed = [
        jnp.where(odd, before, now)
        for before, now in zip([none] + weights + [none], weights + [none, none])
    ]
    first = lax.broadcasted_iota(jnp.int32, (8, blocks), 0) < COMPS
    high_rows = 8 * PAIRS
    table = jnp.concatenate(in_three(octet_rows(table_ref)), axis=0)
    octets = table.shape[1]
    numbers = lax.broadcasted_iota(jnp.int32, (octets, 2 * blocks), 0).astype(jnp.float32).astype(jnp.bfloat16)
    one, zero = jnp.bfloat16(1.0), jnp.bfloat16(0.0)
    for s in range(SLOTS):
        if s % 2 == 0:
            here = jnp.concatenate([octet[s : s + 1], octet[s + 1 : s + 2]], axis=1)
            here = jnp.broadcast_to(here, (16, 2 * blocks)).astype(jnp.bfloat16)
            here = jnp.concatenate([here] * (octets // 16), axis=0)
            two = jnp.dot(table, jnp.where(numbers == here, one, zero), preferred_element_type=jnp.float32)
        got = two[:, s % 2 * blocks : (s % 2 + 1) * blocks]
        got = got[:high_rows] + got[high_rows : 2 * high_rows] + got[2 * high_rows :]
        pairs = [got[8 * a : 8 * a + 8] for a in range(PAIRS)]
        by_four = jnp.broadcast_to(start[s : s + 1], (8, blocks)) & 4 != 0
        by_two = jnp.broadcast_to(start[s : s + 1], (8, blocks)) & 2 != 0
        pairs = [jnp.where(by_four, pairs[a + 2], pairs[a]) for a in range(4)]
        pairs = [jnp.where(by_two, pairs[a + 1], pairs[a]) for a in range(3)]
        both = None
        for a in range(3):
            value = jnp.where(first, placed[2 * a][s : s + 1], placed[2 * a + 1][s : s + 1])
            term = value * pairs[a]
            both = term if both is None else both + term
        both = both + pltpu.roll(both, COMPS, 0)
        for m in range(COMPS):
            quat_ref[m, s : s + 1, :] = both[m : m + 1]

    count = in_order(count_ref)[:1]
    source = in_order(source_ref)[:1]
    slot = lax.broadcasted_iota(jnp.int32, (SLOTS, blocks), 0)
    live = (slot < count).astype(jnp.float32)
    times = to_slot_rows(time_ref[...])
    parallaxes = to_slot_rows(parallax_ref[...]) * live
    observations = to_slot_rows(observed_ref[...])
    totals = [None] * 20
    for at in range(SLOTS // 8):
        here = slice(8 * at, 8 * at + 8)
        q0, q1, q2, q3 = (quat_ref[m, here, :] for m in range(COMPS))
        cross = live[here] * (q0 * q0 + q1 * q1 - q2 * q2 - q3 * q3)
        along = live[here] * (2.0 * (q1 * q2 + q0 * q3))
        tilt = 2.0 * (q1 * q3 - q0 * q2)
        time = times[here]
        design = [cross, along, parallaxes[here], time * cross, time * along]
        residual = observations[here] - tilt
        products = [design[i] * design[j] for i, j in PAIR_LIST]
        products += [design[i] * residual for i in range(5)]
        totals = [p if t is None else t + p for t, p in zip(totals, products)]

    within = lax.broadcasted_iota(jnp.int32, (owned, blocks), 0)
    low = (source % owned == within).astype(jnp.float32)
    spread = jnp.concatenate([jnp.sum(t, axis=0, keepdims=True) * low for t in totals], axis=0)
    owner = (lax.broadcasted_iota(jnp.int32, (owners, blocks), 0) + TM_ORDER[0]) % owners
    high = (source // owned == owner).astype(jnp.float32).astype(jnp.bfloat16)
    result = None
    for piece in in_three(spread):
        got = lax.dot_general(
            high, piece, (((1,), (1,)), ((), ())), preferred_element_type=jnp.float32
        )
        result = got if result is None else result + got
    for j in range(out_ref.shape[0]):
        out_ref[j] = result[j : j + 1]


def solve_kernel(parts_ref, prior_ref, out_ref):
    owned = prior_ref.shape[1]
    total = jnp.sum(parts_ref[...], axis=0)
    total = jnp.broadcast_to(total, (8, total.shape[1]))
    tiles = [total[:, :LANES], jnp.concatenate([total[:, LANES:], total[:, : 2 * LANES - total.shape[1]]], axis=1)]
    normal = []
    for p in range(20):
        tile, lane = divmod(owned * p, LANES)
        normal.append(pltpu.roll(tiles[tile], LANES - lane, 1) if lane else tiles[tile])
    entry = {}
    for index, (i, j) in enumerate(PAIR_LIST):
        entry[j, i] = normal[index]
    for i in range(5):
        own = jnp.broadcast_to(prior_ref[i : i + 1, :], (8, owned))
        entry[i, i] = entry[i, i] + jnp.concatenate([own] * (LANES // owned), axis=1)
    right = normal[15:]
    lower = {}
    inverse = []
    for col in range(5):
        inverse.append(1.0 / entry[col, col])
        for row in range(col + 1, 5):
            lower[row, col] = entry[row, col] * inverse[col]
        for row in range(col + 1, 5):
            for other in range(col + 1, row + 1):
                entry[row, other] = entry[row, other] - lower[row, col] * entry[other, col]
            right[row] = right[row] - lower[row, col] * right[col]
    result = [None] * 5
    for i in range(4, -1, -1):
        value = right[i] * inverse[i]
        for k in range(i + 1, 5):
            value = value - lower[k, i] * result[k]
        result[i] = value
        out_ref[i : i + 1, :] = value[:1, :owned]


def exchanged(array, axis, order):
    return lax.all_to_all(array, axis, 0, 0, axis_index_groups=[order], tiled=True)


def on_device(
    attitude,
    slot_time,
    slot_parallax,
    slot_observed,
    slot_phase,
    slot_knot,
    block_source,
    block_count,
    prior,
):
    n_sky = lax.axis_size("sky")
    n_tm = lax.axis_size("tm")
    shard = attitude[:, 0, :]
    blocks = block_source.shape[0]
    owned = prior.shape[1]
    f32 = jnp.float32

    def rows(array):
        return array.reshape(-1, LANES)

    given = [attitude] + [
        rows(array)
        for array in (
            slot_phase, slot_knot, block_source, block_count, slot_time, slot_parallax, slot_observed,
        )
    ]
    copies, *here = pl.pallas_call(
        fetch_kernel,
        out_shape=[jax.ShapeDtypeStruct((n_sky, *shard.shape), f32)]
        + [jax.ShapeDtypeStruct(array.shape, array.dtype) for array in given[1:]],
        in_specs=[pl.BlockSpec(memory_space=pltpu.HBM)] * len(given),
        scratch_shapes=[pltpu.VMEM(attitude.shape, f32), pltpu.SemaphoreType.DMA((len(given),))],
        compiler_params=pltpu.CompilerParams(vmem_limit_bytes=4 << 20),
        name="fetch",
    )(*[pltpu.with_memory_space_constraint(array, pltpu.HBM) for array in given])
    table = exchanged(copies, "sky", SKY_ORDER)
    partial = pl.pallas_call(
        sums_kernel,
        out_shape=jax.ShapeDtypeStruct((n_tm, 1, 20 * owned), f32),
        scratch_shapes=[pltpu.VMEM((COMPS, SLOTS, blocks), f32)],
        compiler_params=pltpu.CompilerParams(vmem_limit_bytes=16 << 20),
        name="sums",
    )(table, *here)
    parts = exchanged(partial, "tm", TM_ORDER)
    return pl.pallas_call(
        solve_kernel,
        out_shape=jax.ShapeDtypeStruct((5, owned), f32),
        compiler_params=pltpu.CompilerParams(vmem_limit_bytes=1 << 20),
        name="solve",
    )(parts, prior)


def solution(mesh):
    in_specs = (
        P(None, "tm", "sky"),
        P(("sky", "tm")),
        P(("sky", "tm")),
        P(("sky", "tm")),
        P(("sky", "tm")),
        P(("sky", "tm")),
        P(("sky", "tm")),
        P(("sky", "tm")),
        P(None, ("sky", "tm")),
    )
    out_specs = P(None, ("sky", "tm"))
    return jax.shard_map(
        on_device, mesh=mesh, in_specs=in_specs, out_specs=out_specs, check_vma=False
    )
```
